32 devices in a mesh: seg: 4 (over y, x), bin: 8 (over z, core).
Axes of the slice: x: 2, y: 2, z: 4, core: 2. Of those that a mesh axis runs over, the one named last changes fastest.
Arguments:
- coverage_lanes: bfloat16 [256, 128, 128], P(('seg', 'bin')), may hold values from 4 to 64
- target_blocks: int32 [256], P(('seg', 'bin')), may hold values from 0 to 7, as said below
- valid_bins: int32 [256], P(('seg', 'bin')), may hold values from 1 to 128
- panel_mean: float32 [32768], P(('seg', 'bin')), may hold values from 3.5 to 5
- components: float32 [256, 32768], P(None, ('seg', 'bin')), as said below
- kernels: float32 [3, 33, 32768], P(None, None, ('seg', 'bin')), may hold values from 0 to 0.08
- chrom_starts: int32 [24], replicated, may hold values from 0 to 32767, as said below
Outputs:
- coefficients: float32 [128, 256], replicated
- smoothed: float32 [128, 32768], P(None, ('seg', 'bin'))
- bridge: float32 [128, 32768], P(None, ('seg', 'bin'))
The draws below stay inside these ranges and needn't reach their ends.
Inputs may be any that keep to these rules, and one draw needn't show every extreme that they name: target_blocks names one of the owner's 8 blocks; slot r of a device goes to the owner given by r // 1 within the device's stretch. `chrom_starts`: strictly rising chromosome starts, the first is 0 and the last is 32767. panel-of-normals components.
All inputs are finite; a program needn't handle non-finite values.
Results may differ from the reference program's by a relative error of at most 0.0003.
Values may be sent and summed in bfloat16 or wider, within the bound.
A program may use at most 192 MiB of HBM per device.

```python
import math
import jax
import jax.numpy as jnp
from jax import lax

SAMPLES = 128
COMPONENTS = 256
TAPS = 33
NCONV = 3
BLOCK = 128
NCHROM = 24
BLK_DEV = 8
CAP = 1
HALF = 16
BINS = 32768
LANE_SLOTS = 256
N_SEG = 4
N_BIN = 8


def draw_target_blocks(key, part):
    picks = jax.random.randint(jax.random.fold_in(key, 11), (LANE_SLOTS,), 0, BLK_DEV, dtype=jnp.int32)
    picks = picks.at[0].set(BLK_DEV - 1)
    return picks.at[1].set(0)


def draw_valid_bins(key, part):
    picks = jax.random.randint(jax.random.fold_in(key, 23), (LANE_SLOTS,), 1, BLOCK + 1, dtype=jnp.int32)
    picks = picks.at[0].set(BLOCK)
    return picks.at[1].set(1)


def draw_components(key, part):
    key_noise = jax.random.fold_in(key, 37)
    noise = jax.random.normal(key_noise, (COMPONENTS, BINS), jnp.float32)
    return noise * (1.0 / math.sqrt(BINS))


def draw_chrom_starts(key, part):
    shuffled = jax.random.permutation(jax.random.fold_in(key, 53), BINS - 2)[:NCHROM - 2] + 1
    inner = jnp.sort(shuffled).astype(jnp.int32)
    return jnp.concatenate([jnp.zeros((1,), jnp.int32), inner, jnp.full((1,), BINS - 1, jnp.int32)])


def level_of(stream_key, extent, pieces, least, largest):
    level = 1.0
    for axis_at, blocks in pieces:
        draws = jax.random.uniform(jax.random.fold_in(jax.random.fold_in(stream_key, 6), axis_at), (blocks,), jnp.float32, least / len(pieces), largest / len(pieces))
        level = level * jnp.repeat(jnp.exp(draws), extent[axis_at] // blocks).reshape((-1,) + (1,) * (len(extent) - 1 - axis_at))
    return level


def setup_inputs(seed: int = 0) -> dict:
    seeds = jax.random.split(jax.random.key(seed), 8)
    return {
        "coverage_lanes": jnp.clip(jnp.exp(math.log(64.0) - 2.7725887 * jax.random.uniform(seeds[0], (LANE_SLOTS, SAMPLES, BLOCK), jnp.float32) ** level_of(seeds[0], (LANE_SLOTS, SAMPLES, BLOCK), ((0, 32),), -0.2, 0.2)), 4.0, 64.0).astype(jnp.bfloat16),
        "target_blocks": draw_target_blocks(jax.random.fold_in(seeds[7], 71), 0),
        "valid_bins": draw_valid_bins(jax.random.fold_in(seeds[7], 71), 0),
        "panel_mean": jnp.clip(3.5 + 1.5 * jax.random.uniform(seeds[3], (BINS,), jnp.float32) ** level_of(seeds[3], (BINS,), ((0, 32),), -0.2, 0.2), 3.5, 5.0),
        "components": draw_components(jax.random.fold_in(seeds[7], 71), 0),
        "kernels": jnp.clip(0.08 * jax.random.uniform(seeds[5], (NCONV, TAPS, BINS), jnp.float32) ** level_of(seeds[5], (NCONV, TAPS, BINS), ((2, 32),), -0.2, 0.2), 0.0, 0.08),
        "chrom_starts": draw_chrom_starts(jax.random.fold_in(seeds[7], 71), 0),
    }


def chrom_labels(chrom_starts, first_bin, count, total_bins):
    positions = first_bin + jnp.arange(count, dtype=jnp.int32)
    covered = lax.optimization_barrier(jnp.sum((chrom_starts[:, None] <= positions[None, :]).astype(jnp.int32), axis=0)) - 1
    return jnp.where(positions >= total_bins, chrom_starts.shape[0], covered)

def smooth_once(padded, tap_weights, labels, out_width):
    half_taps = (tap_weights.shape[0] - 1) // 2
    centre = labels[half_taps:half_taps + out_width]
    result = jnp.zeros((padded.shape[0], out_width), jnp.float32)
    for tap_index in range(tap_weights.shape[0]):
        weight = tap_weights[tap_index] * (labels[tap_index:tap_index + out_width] == centre).astype(jnp.float32)
        result = result + weight[None, :] * padded[:, tap_index:tap_index + out_width]
    return result

def reference(coverage_lanes, target_blocks, valid_bins, panel_mean, components, kernels, chrom_starts):
    per_device = N_BIN * CAP
    slot_ids = jnp.arange(LANE_SLOTS, dtype=jnp.int32)
    sender = slot_ids // per_device
    owner = sender // N_BIN * N_BIN + slot_ids % per_device // CAP
    block_ids = (owner * BLK_DEV + target_blocks).astype(jnp.int32)
    keep_mask = (jnp.arange(BLOCK, dtype=jnp.int32)[None, :] < valid_bins[:, None]).astype(jnp.bfloat16)

    def add_device(device_index, gathered):
        start = (device_index * per_device).astype(jnp.int32)
        rows = lax.dynamic_slice_in_dim(coverage_lanes, start, per_device, 0)
        masks = lax.dynamic_slice_in_dim(keep_mask, start, per_device, 0)
        places = lax.dynamic_slice_in_dim(block_ids, start, per_device, 0)
        masked = (rows * masks[:, None, :]).astype(jnp.float32)
        return gathered.at[places].add(masked)
    gathered = lax.fori_loop(0, N_SEG * N_BIN, add_device, jnp.zeros((BINS // BLOCK, SAMPLES, BLOCK), jnp.float32))
    coverage = jnp.transpose(gathered, (1, 0, 2)).reshape(SAMPLES, BINS)
    log_ratio = jnp.log(coverage + 1.0) - panel_mean[None, :]
    coefficients = jnp.dot(log_ratio, components.T, precision=lax.Precision.HIGHEST, preferred_element_type=jnp.float32)
    signal = log_ratio - jnp.dot(coefficients, components, precision=lax.Precision.HIGHEST, preferred_element_type=jnp.float32)
    labels = chrom_labels(chrom_starts, -HALF, BINS + 2 * HALF, BINS)
    smoothed = signal
    for layer_index in range(NCONV):
        padded = jnp.pad(smoothed, ((0, 0), (HALF, HALF)))
        smoothed = smooth_once(padded, kernels[layer_index], labels, BINS)
    mean_level = lax.optimization_barrier(jnp.sum(smoothed, axis=1)) / BINS
    bridge = jnp.cumsum(smoothed - mean_level[:, None], axis=1) * (1.0 / math.sqrt(BINS))
    return (coefficients, smoothed, bridge)
```

```python
import functools
import math

import jax
import jax.numpy as jnp
from jax import lax
from jax.experimental import pallas as pl
from jax.experimental.pallas import tpu as pltpu
from jax.sharding import PartitionSpec as P

MESH = pl.DeviceIdType.MESH
F32, BF16 = jnp.float32, jnp.bfloat16
LANES = 128


def split(x):
    high = x.astype(BF16)
    return high, (x - high.astype(F32)).astype(BF16)


def mm(a, b, contract=(1, 0)):
    return lax.dot_general(
        a, b, (((contract[0],), (contract[1],)), ((), ())), preferred_element_type=F32
    )


def iota(shape, dim):
    return lax.broadcasted_iota(jnp.int32, shape, dim)


def wait_bytes(ref, sem):
    pltpu.make_async_copy(ref, ref, sem).wait()


def body(
    nseg, nb, targets, valid, starts, lanes, panel, comp, kern,
    coef_o, smooth_o, bridge_o,
    send_l, recv_l, kx, taps, lrx, kh, kl, lh, ll, ah, al, bh, bl,
    skh, skl, weights, part, gathered, c2, sums, ssem, rsem, lsem,
):
    ndev = nseg * nb
    seg, place = lax.axis_index("seg"), lax.axis_index("bin")
    me = seg * nb + place
    samples, bin_dev = smooth_o.shape
    comps = kx.shape[0]
    blocks = bin_dev // LANES
    total_bins = bin_dev * ndev
    first = me * bin_dev
    ntaps = kern.shape[1]
    half = (ntaps - 1) // 2

    def dev(flat):
        return (lax.div(flat, nb), lax.rem(flat, nb))

    def remote(src, dst, which, device):
        return pltpu.make_async_remote_copy(
            src_ref=src, dst_ref=dst, send_sem=ssem.at[which], recv_sem=rsem.at[which],
            device_id=device, device_id_type=MESH,
        )

    barrier = pltpu.get_barrier_semaphore()

    @pl.loop(1, ndev)
    def _(hop):
        pl.semaphore_signal(
            barrier, inc=1, device_id=dev(lax.rem(me + hop, ndev)), device_id_type=MESH
        )

    own_k = pltpu.make_async_copy(comp, kx.at[:, pl.ds(LANES, bin_dev)], lsem.at[0])
    own_k.start()
    own_t = pltpu.make_async_copy(kern, taps.at[:, :, pl.ds(LANES, bin_dev)], lsem.at[1])
    own_t.start()

    @pl.loop(0, nb)
    def _(r):
        keep = iota((samples, LANES), 1) < valid[r]
        send_l[r, :samples, :] = jnp.where(keep, lanes[r].astype(F32), 0.0).astype(BF16)
        mark = jnp.full((16, LANES), targets[r], jnp.int32).astype(F32)
        send_l[r, samples:, :] = mark.astype(BF16)

    pl.semaphore_wait(barrier, ndev - 1)

    @pl.loop(1, nb)
    def _(hop):
        to = lax.rem(place + hop, nb)
        remote(send_l.at[to], recv_l.at[place], 0, (seg, to)).start()

    right, left = dev(lax.rem(me + 1, ndev)), dev(lax.rem(me + ndev - 1, ndev))
    low, high = pl.ds(0, LANES), pl.ds(bin_dev + LANES, LANES)
    head, tail = pl.ds(0, LANES), pl.ds(bin_dev - LANES, LANES)
    halos = [
        remote(kern.at[pl.ds(0, 2), :, tail], taps.at[pl.ds(0, 2), :, low], 1, right),
        remote(kern.at[pl.ds(0, 2), :, head], taps.at[pl.ds(0, 2), :, high], 2, left),
        remote(comp.at[:, tail], kx.at[:, low], 3, right),
        remote(comp.at[:, head], kx.at[:, high], 4, left),
    ]
    for copy in halos:
        copy.start()

    recv_l[place] = send_l[place]

    own_t.wait()
    halos[0].wait_recv()
    halos[1].wait_recv()

    def band(layer, m, offset, top):
        if offset == LANES:
            columns = pl.ds(pl.multiple_of((m + 1) * LANES, LANES), LANES)
            upper = taps[layer, : 2 * half, columns]
            last = taps[layer, 2 * half : ntaps, columns]
        else:
            columns = pl.ds(pl.multiple_of(m * LANES, LANES), 2 * LANES)
            upper = taps[layer, : 2 * half, columns]
            last = taps[layer, 2 * half : ntaps, columns]
        last = jnp.broadcast_to(last, (8, last.shape[1]))
        last = jnp.where(iota(last.shape, 0) == 0, last, 0.0)
        rows = jnp.concatenate([upper, last], axis=0)
        if offset != LANES:
            rows = pltpu.roll(rows, 2 * LANES - offset, 1)[:, :LANES]
        position = first - LANES + offset + m * LANES + iota((8, LANES), 1)
        lower = jnp.full((8, LANES), total_bins, jnp.int32)
        upto = jnp.where(position < total_bins, total_bins, -1)
        count = starts.shape[0]
        for k in range(count):
            lower = jnp.where(starts[k] <= position, starts[k], lower)
        for k in range(count - 1, -1, -1):
            upto = jnp.where(starts[k] > position, starts[k], upto)
        tall = rows.shape[0]
        source = position[:1] + iota((tall, LANES), 0) - half
        inside = (source >= lower[:1]) & (source < upto[:1])
        rows = jnp.where(inside, rows, 0.0)
        lane = iota((1, LANES), 1)
        step = 1
        while step < LANES:
            if step < 8:
                moved = pltpu.roll(rows, step, 0)
                still = rows
            else:
                pad = jnp.zeros((step, LANES), F32)
                moved = jnp.concatenate([pad, rows], axis=0)
                still = jnp.concatenate([rows, pad], axis=0)
            chosen = jnp.broadcast_to((lane & step) != 0, moved.shape)
            rows = jnp.where(chosen, moved, still)
            step *= 2
        rest = 2 * LANES - rows.shape[0] - top
        pieces = [rows, jnp.zeros((rest, LANES), F32)]
        if top:
            pieces = [jnp.zeros((top, LANES), F32)] + pieces
        return split(jnp.concatenate(pieces, axis=0))

    plan = (
        (0, LANES - 2 * half, LANES - 3 * half, 0, blocks + 1),
        (1, LANES - half, 0, blocks + 1, blocks + 1),
        (2, LANES, 0, 2 * blocks + 2, blocks),
    )
    for layer, offset, top, base, many in plan:

        @pl.loop(0, many)
        def _(m, layer=layer, offset=offset, top=top, base=base):
            w_high, w_low = band(layer, m, offset, top)
            weights[base + m, :, :LANES] = w_high
            weights[base + m, :, LANES:] = w_low

    def smooth_pass(src_high, src_low, m, base):
        window = pl.ds(m * LANES, 2 * LANES)
        both = mm(src_high[:, window], weights[base + m])
        return both[:, :LANES] + both[:, LANES:] + mm(
            src_low[:, window], weights[base + m, :, :LANES]
        )

    def smooth(src, mid, end, rows, store):
        for m in range(blocks + 1):
            out = split(smooth_pass(src[0], src[1], m, plan[0][3]))
            for ref, value in zip(mid, out):
                ref[:rows, pl.ds(m * LANES, LANES)] = value
        for m in range(blocks + 1):
            out = split(
                smooth_pass(mid[0].at[:rows], mid[1].at[:rows], m, plan[1][3])
            )
            for ref, value in zip(end, out):
                ref[:rows, pl.ds(m * LANES, LANES)] = value
        total = jnp.zeros((rows, LANES), F32)
        for m in range(blocks):
            out = smooth_pass(end[0].at[:rows], end[1].at[:rows], m, plan[2][3])
            store(m, out)
            total = total + out
        return jnp.sum(total, axis=1, keepdims=True)

    eye = iota((LANES, LANES), 0) == iota((LANES, LANES), 1)

    def as_row(column):
        return jnp.sum(jnp.where(eye, column, 0.0), axis=0, keepdims=True)

    own_k.wait()
    halos[2].wait_recv()
    halos[3].wait_recv()
    for ref in (ah, al, bh, bl):
        ref[:, pl.ds(bin_dev + LANES, LANES)] = jnp.zeros((comps, LANES), BF16)
    kh[...], kl[...] = split(kx[...])

    def store_k(m, out):
        window = pl.ds(m * LANES, LANES)
        skh[:, window], skl[:, window] = split(out)

    k_total = smooth((kh, kl), (ah, al), (bh, bl), comps, store_k)

    wait_bytes(recv_l.at[pl.ds(0, nb - 1)], rsem.at[0])
    for b in range(blocks):

        def add(r, acc):
            mark = recv_l[r, samples : samples + 16, :].astype(F32)[:1]
            return acc + jnp.where(
                jnp.broadcast_to(mark == float(b), acc.shape),
                recv_l[r, :samples, :].astype(F32), 0.0,
            )

        cover = lax.fori_loop(0, nb, add, jnp.zeros((samples, LANES), F32), unroll=nb <= 8)
        window = pl.ds(b * LANES, LANES)
        lrx[:, pl.ds((b + 1) * LANES, LANES)] = jnp.log(cover + 1.0) - panel[:, window]

    near = [
        remote(lrx.at[:, pl.ds(bin_dev, LANES)], lrx.at[:, low], 5, right),
        remote(lrx.at[:, pl.ds(LANES, LANES)], lrx.at[:, high], 6, left),
    ]
    for copy in near:
        copy.start()

    own = pl.ds(LANES, bin_dev)
    lh[:, own], ll[:, own] = split(lrx[:, own])
    terms = (
        mm(lh[:, own], kh[:, own], (1, 1))
        + mm(ll[:, own], kh[:, own], (1, 1))
        + mm(lh[:, own], kl[:, own], (1, 1))
    )
    for h in range(comps // LANES):
        part[pl.ds(h * samples, samples), :] = terms[:, h * LANES : (h + 1) * LANES]

    tiles = part.shape[0] // 8
    stride = ndev // tiles
    mine = lax.div(me, stride)
    owner = lax.rem(me, stride) == 0

    def tile(j):
        return pl.ds(pl.multiple_of(j * 8, 8), 8)

    @pl.loop(1 if stride == 1 else 0, tiles)
    def _(hop):
        j = lax.rem(mine + hop, tiles)
        copy = remote(part.at[tile(j)], gathered.at[me], 7, dev(j * stride))
        if stride == 1:
            copy.start()
        else:
            pl.when(j * stride != me)(copy.start)

    for copy in near:
        copy.wait_recv()
    for edge in (low, high):
        lh[:, edge], ll[:, edge] = split(lrx[:, edge])

    def store_l(m, out):
        smooth_o[:, pl.ds(m * LANES, LANES)] = out

    l_total = smooth((lh, ll), (ah, al), (bh, bl), samples, store_l)
    sums[me] = jnp.concatenate(
        [as_row(l_total)]
        + [as_row(k_total[h * LANES : (h + 1) * LANES]) for h in range(comps // LANES)]
        + [jnp.zeros((7 - comps // LANES, LANES), F32)],
        axis=0,
    )

    def reduce_and_send():
        gathered[me] = part[tile(mine), :]
        wait_bytes(gathered.at[pl.ds(0, ndev - 1)], rsem.at[7])
        c2[tile(mine), :] = jnp.sum(gathered[...], axis=0)

        @pl.loop(1, ndev)
        def _(hop):
            to = dev(lax.rem(me + hop, ndev))
            remote(c2.at[tile(mine)], c2.at[tile(mine)], 8, to).start()

    if stride == 1:
        reduce_and_send()
    else:
        pl.when(owner)(reduce_and_send)

    @pl.loop(1, ndev)
    def _(hop):
        remote(sums.at[me], sums.at[me], 9, dev(lax.rem(me + hop, ndev))).start()

    if stride == 1:
        wait_bytes(c2.at[pl.ds(0, 8 * (tiles - 1))], rsem.at[8])
    else:

        @pl.when(owner)
        def _():
            wait_bytes(c2.at[pl.ds(0, 8 * (tiles - 1))], rsem.at[8])

        @pl.when(jnp.logical_not(owner))
        def _():
            wait_bytes(c2, rsem.at[8])

    coef = jnp.concatenate(
        [c2[pl.ds(h * samples, samples), :] for h in range(comps // LANES)], axis=1
    )
    coef_o[...] = coef
    c_high, c_low = split(coef)
    smooth_o[...] = smooth_o[...] - (
        mm(c_high, skh[...]) + mm(c_low, skh[...]) + mm(c_high, skl[...])
    )

    wait_bytes(sums.at[pl.ds(0, ndev - 1)], rsem.at[9])
    every = jnp.sum(sums[...], axis=0)
    part_mean = every * (1.0 / ndev)

    def earlier(q, acc):
        return acc + jnp.where(q < me, 1.0, 0.0) * (sums[q] - part_mean)

    before_rows = lax.fori_loop(0, ndev, earlier, jnp.zeros((8, LANES), F32), unroll=ndev <= 32)

    def resolve(rows):
        level = jnp.where(eye, jnp.broadcast_to(rows[:1], (LANES, LANES)), 0.0)
        for h in range(comps // LANES):
            level = level - coef[:, h * LANES : (h + 1) * LANES] * rows[h + 1 : h + 2]
        return jnp.sum(level, axis=1, keepdims=True)

    mean = resolve(part_mean) * (1.0 / bin_dev)
    carry = resolve(before_rows)
    wide = 2 * LANES
    ones = jnp.where(iota((wide, wide), 0) <= iota((wide, wide), 1), 1.0, 0.0).astype(BF16)
    scale = 1.0 / math.sqrt(total_bins)
    for m in range(bin_dev // wide):
        window = pl.ds(m * wide, wide)
        v_high, v_low = split(smooth_o[:, window] - mean)
        run = mm(v_high, ones) + mm(v_low, ones) + carry
        bridge_o[:, window] = run * scale
        carry = run[:, wide - 1 :]

    wait_bytes(send_l.at[pl.ds(0, nb - 1)], ssem.at[0])
    for copy in halos + near:
        copy.wait_send()
    wait_bytes(sums.at[pl.ds(0, ndev - 1)], ssem.at[9])
    if stride == 1:
        wait_bytes(part.at[pl.ds(0, 8 * (tiles - 1))], ssem.at[7])
        wait_bytes(gathered.at[pl.ds(0, ndev - 1)], ssem.at[8])
    else:

        @pl.when(owner)
        def _():
            wait_bytes(part.at[pl.ds(0, 8 * (tiles - 1))], ssem.at[7])
            wait_bytes(gathered.at[pl.ds(0, ndev - 1)], ssem.at[8])

        @pl.when(jnp.logical_not(owner))
        def _():
            wait_bytes(part, ssem.at[7])


def solution(mesh):
    nseg, nb = mesh.shape["seg"], mesh.shape["bin"]
    ndev = nseg * nb

    def per_device(lanes, targets, valid, panel, comp, kern, starts):
        samples = lanes.shape[1]
        comps, bin_dev = comp.shape
        layers, ntaps = kern.shape[:2]
        ext = bin_dev + 2 * LANES
        bands = 3 * (bin_dev // LANES) + 2
        vmem, smem = pltpu.VMEM, pltpu.SMEM
        whole = pl.BlockSpec(memory_space=vmem)
        scalar = pl.BlockSpec(memory_space=smem)
        away = pl.BlockSpec(memory_space=pl.ANY)
        return pl.pallas_call(
            functools.partial(body, nseg, nb),
            out_shape=(
                jax.ShapeDtypeStruct((samples, comps), F32),
                jax.ShapeDtypeStruct((samples, bin_dev), F32),
                jax.ShapeDtypeStruct((samples, bin_dev), F32),
            ),
            in_specs=[scalar, scalar, scalar, whole, whole, away, away],
            out_specs=(whole, whole, whole),
            scratch_shapes=[
                vmem((nb, samples + 16, LANES), BF16),
                vmem((nb, samples + 16, LANES), BF16),
                vmem((comps, ext), F32),
                vmem((layers, ntaps, ext), F32),
                vmem((samples, ext), F32),
                vmem((comps, ext), BF16),
                vmem((comps, ext), BF16),
                vmem((samples, ext), BF16),
                vmem((samples, ext), BF16),
                vmem((comps, ext), BF16),
                vmem((comps, ext), BF16),
                vmem((comps, ext), BF16),
                vmem((comps, ext), BF16),
                vmem((comps, bin_dev), BF16),
                vmem((comps, bin_dev), BF16),
                vmem((bands, 2 * LANES, 2 * LANES), BF16),
                vmem((samples * comps // LANES, LANES), F32),
                vmem((ndev, 8, LANES), F32),
                vmem((samples * comps // LANES, LANES), F32),
                vmem((ndev, 8, LANES), F32),
                pltpu.SemaphoreType.DMA((10,)),
                pltpu.SemaphoreType.DMA((10,)),
                pltpu.SemaphoreType.DMA((2,)),
            ],
            compiler_params=pltpu.CompilerParams(
                collective_id=0, has_side_effects=True, vmem_limit_bytes=48 << 20
            ),
        )(targets, valid, starts, lanes, panel.reshape(1, bin_dev), comp, kern)

    in_specs = (
        P(("seg", "bin"), None, None),
        P(("seg", "bin")),
        P(("seg", "bin")),
        P(("seg", "bin")),
        P(None, ("seg", "bin")),
        P(None, None, ("seg", "bin")),
        P(),
    )
    out_specs = (P(), P(None, ("seg", "bin")), P(None, ("seg", "bin")))
    return jax.shard_map(
        per_device, mesh=mesh, in_specs=in_specs, out_specs=out_specs, check_vma=False
    )
```

```python
import functools
import math

import jax
import jax.numpy as jnp
from jax import lax
from jax.experimental import pallas as pl
from jax.experimental.pallas import tpu as pltpu
from jax.sharding import PartitionSpec as P

MESH = pl.DeviceIdType.MESH
F32, BF16 = jnp.float32, jnp.bfloat16
LANES = 128


def split(x):
    high = x.astype(BF16)
    return high, (x - high.astype(F32)).astype(BF16)


def mm(a, b, contract=(1, 0)):
    return lax.dot_general(
        a, b, (((contract[0],), (contract[1],)), ((), ())), preferred_element_type=F32
    )


def iota(shape, dim):
    return lax.broadcasted_iota(jnp.int32, shape, dim)


def wait_bytes(ref, sem):
    pltpu.make_async_copy(ref, ref, sem).wait()


def body(
    nseg, nb, targets_h, valid_h, starts_h, lanes_h, panel_h, comp, kern,
    coef_o, smooth_o, skh, skl, level_o,
    targets, valid, starts, lanes, panel,
    send_l, recv_l, kx, taps, lrx, kh, kl, lh, ll, ah, al, bh, bl,
    weights, part, gathered, c2, sums, ssem, rsem, lsem,
):
    ndev = nseg * nb
    seg, place = lax.axis_index("seg"), lax.axis_index("bin")
    me = seg * nb + place
    samples, bin_dev = smooth_o.shape
    comps = kx.shape[0]
    blocks = bin_dev // LANES
    total_bins = bin_dev * ndev
    first = me * bin_dev
    ntaps = kern.shape[1]
    half = (ntaps - 1) // 2

    def dev(flat):
        return (lax.div(flat, nb), lax.rem(flat, nb))

    def remote(src, dst, which, device):
        return pltpu.make_async_remote_copy(
            src_ref=src, dst_ref=dst, send_sem=ssem.at[which], recv_sem=rsem.at[which],
            device_id=device, device_id_type=MESH,
        )

    barrier = pltpu.get_barrier_semaphore()

    @pl.loop(1, ndev)
    def _(hop):
        pl.semaphore_signal(
            barrier, inc=1, device_id=dev(lax.rem(me + hop, ndev)), device_id_type=MESH
        )

    fetched = [
        pltpu.make_async_copy(src, dst, lsem.at[i + 2])
        for i, (src, dst) in enumerate(
            (
                (valid_h, valid), (targets_h, targets), (lanes_h, lanes),
                (starts_h, starts), (panel_h, panel),
            )
        )
    ]
    for copy in fetched:
        copy.start()
    own_k = pltpu.make_async_copy(comp, kx.at[:, pl.ds(LANES, bin_dev)], lsem.at[0])
    own_k.start()
    own_t = pltpu.make_async_copy(kern, taps.at[:, :, pl.ds(LANES, bin_dev)], lsem.at[1])
    own_t.start()

    for copy in fetched:
        copy.wait()

    @pl.loop(0, nb)
    def _(r):
        keep = iota((samples, LANES), 1) < valid[r]
        send_l[r, :samples, :] = jnp.where(keep, lanes[r].astype(F32), 0.0).astype(BF16)
        mark = jnp.full((16, LANES), targets[r], jnp.int32).astype(F32)
        send_l[r, samples:, :] = mark.astype(BF16)

    pl.semaphore_wait(barrier, ndev - 1)

    @pl.loop(1, nb)
    def _(hop):
        to = lax.rem(place + hop, nb)
        remote(send_l.at[to], recv_l.at[place], 0, (seg, to)).start()

    right, left = dev(lax.rem(me + 1, ndev)), dev(lax.rem(me + ndev - 1, ndev))
    low, high = pl.ds(0, LANES), pl.ds(bin_dev + LANES, LANES)
    head, tail = pl.ds(0, LANES), pl.ds(bin_dev - LANES, LANES)
    halos = [
        remote(kern.at[pl.ds(0, 2), :, tail], taps.at[pl.ds(0, 2), :, low], 1, right),
        remote(kern.at[pl.ds(0, 2), :, head], taps.at[pl.ds(0, 2), :, high], 2, left),
        remote(comp.at[:, tail], kx.at[:, low], 3, right),
        remote(comp.at[:, head], kx.at[:, high], 4, left),
    ]
    for copy in halos:
        copy.start()

    recv_l[place] = send_l[place]

    own_t.wait()
    halos[0].wait_recv()
    halos[1].wait_recv()

    def band(layer, m, offset, top):
        if offset == LANES:
            columns = pl.ds(pl.multiple_of((m + 1) * LANES, LANES), LANES)
            upper = taps[layer, : 2 * half, columns]
            last = taps[layer, 2 * half : ntaps, columns]
        else:
            columns = pl.ds(pl.multiple_of(m * LANES, LANES), 2 * LANES)
            upper = taps[layer, : 2 * half, columns]
            last = taps[layer, 2 * half : ntaps, columns]
        last = jnp.broadcast_to(last, (8, last.shape[1]))
        last = jnp.where(iota(last.shape, 0) == 0, last, 0.0)
        rows = jnp.concatenate([upper, last], axis=0)
        if offset != LANES:
            rows = pltpu.roll(rows, 2 * LANES - offset, 1)[:, :LANES]
        position = first - LANES + offset + m * LANES + iota((8, LANES), 1)
        lower = jnp.full((8, LANES), total_bins, jnp.int32)
        upto = jnp.where(position < total_bins, total_bins, -1)
        count = starts.shape[0]
        for k in range(count):
            lower = jnp.where(starts[k] <= position, starts[k], lower)
        for k in range(count - 1, -1, -1):
            upto = jnp.where(starts[k] > position, starts[k], upto)
        tall = rows.shape[0]
        source = position[:1] + iota((tall, LANES), 0) - half
        inside = (source >= lower[:1]) & (source < upto[:1])
        rows = jnp.where(inside, rows, 0.0)
        lane = iota((1, LANES), 1)
        step = 1
        while step < LANES:
            if step < 8:
                moved = pltpu.roll(rows, step, 0)
                still = rows
            else:
                pad = jnp.zeros((step, LANES), F32)
                moved = jnp.concatenate([pad, rows], axis=0)
                still = jnp.concatenate([rows, pad], axis=0)
            chosen = jnp.broadcast_to((lane & step) != 0, moved.shape)
            rows = jnp.where(chosen, moved, still)
            step *= 2
        rest = 2 * LANES - rows.shape[0] - top
        pieces = [rows, jnp.zeros((rest, LANES), F32)]
        if top:
            pieces = [jnp.zeros((top, LANES), F32)] + pieces
        return split(jnp.concatenate(pieces, axis=0))

    plan = (
        (0, LANES - 2 * half, LANES - 3 * half, 0, blocks + 1),
        (1, LANES - half, 0, blocks + 1, blocks + 1),
        (2, LANES, 0, 2 * blocks + 2, blocks),
    )
    for layer, offset, top, base, many in plan:

        @pl.loop(0, many)
        def _(m, layer=layer, offset=offset, top=top, base=base):
            w_high, w_low = band(layer, m, offset, top)
            weights[base + m, :, :LANES] = w_high
            weights[base + m, :, LANES:] = w_low

    def smooth_pass(src_high, src_low, m, base):
        window = pl.ds(m * LANES, 2 * LANES)
        both = mm(src_high[:, window], weights[base + m])
        return both[:, :LANES] + both[:, LANES:] + mm(
            src_low[:, window], weights[base + m, :, :LANES]
        )

    def smooth(src, mid, end, rows, store):
        for m in range(blocks + 1):
            out = split(smooth_pass(src[0], src[1], m, plan[0][3]))
            for ref, value in zip(mid, out):
                ref[:rows, pl.ds(m * LANES, LANES)] = value
        for m in range(blocks + 1):
            out = split(
                smooth_pass(mid[0].at[:rows], mid[1].at[:rows], m, plan[1][3])
            )
            for ref, value in zip(end, out):
                ref[:rows, pl.ds(m * LANES, LANES)] = value
        total = jnp.zeros((rows, LANES), F32)
        for m in range(blocks):
            out = smooth_pass(end[0].at[:rows], end[1].at[:rows], m, plan[2][3])
            store(m, out)
            total = total + out
        return jnp.sum(total, axis=1, keepdims=True)

    eye = iota((LANES, LANES), 0) == iota((LANES, LANES), 1)

    def as_row(column):
        return jnp.sum(jnp.where(eye, column, 0.0), axis=0, keepdims=True)

    own_k.wait()
    halos[2].wait_recv()
    halos[3].wait_recv()
    for ref in (ah, al, bh, bl):
        ref[:, pl.ds(bin_dev + LANES, LANES)] = jnp.zeros((comps, LANES), BF16)
    kh[...], kl[...] = split(kx[...])

    def store_k(m, out):
        window = pl.ds(m * LANES, LANES)
        skh[:, window], skl[:, window] = split(out)

    k_total = smooth((kh, kl), (ah, al), (bh, bl), comps, store_k)

    wait_bytes(recv_l.at[pl.ds(0, nb - 1)], rsem.at[0])
    for b in range(blocks):

        def add(r, acc):
            mark = recv_l[r, samples : samples + 16, :].astype(F32)[:1]
            return acc + jnp.where(
                jnp.broadcast_to(mark == float(b), acc.shape),
                recv_l[r, :samples, :].astype(F32), 0.0,
            )

        cover = lax.fori_loop(0, nb, add, jnp.zeros((samples, LANES), F32), unroll=nb <= 8)
        window = pl.ds(b * LANES, LANES)
        lrx[:, pl.ds((b + 1) * LANES, LANES)] = jnp.log(cover + 1.0) - panel[:, window]

    near = [
        remote(lrx.at[:, pl.ds(bin_dev, LANES)], lrx.at[:, low], 5, right),
        remote(lrx.at[:, pl.ds(LANES, LANES)], lrx.at[:, high], 6, left),
    ]
    for copy in near:
        copy.start()

    own = pl.ds(LANES, bin_dev)
    lh[:, own], ll[:, own] = split(lrx[:, own])
    terms = (
        mm(lh[:, own], kh[:, own], (1, 1))
        + mm(ll[:, own], kh[:, own], (1, 1))
        + mm(lh[:, own], kl[:, own], (1, 1))
    )
    for h in range(comps // LANES):
        part[pl.ds(h * samples, samples), :] = terms[:, h * LANES : (h + 1) * LANES]

    tiles = part.shape[0] // 8
    stride = ndev // tiles
    mine = lax.div(me, stride)
    owner = lax.rem(me, stride) == 0

    def tile(j):
        return pl.ds(pl.multiple_of(j * 8, 8), 8)

    @pl.loop(1 if stride == 1 else 0, tiles)
    def _(hop):
        j = lax.rem(mine + hop, tiles)
        copy = remote(part.at[tile(j)], gathered.at[me], 7, dev(j * stride))
        if stride == 1:
            copy.start()
        else:
            pl.when(j * stride != me)(copy.start)

    for copy in near:
        copy.wait_recv()
    for edge in (low, high):
        lh[:, edge], ll[:, edge] = split(lrx[:, edge])

    def store_l(m, out):
        smooth_o[:, pl.ds(m * LANES, LANES)] = out

    l_total = smooth((lh, ll), (ah, al), (bh, bl), samples, store_l)
    sums[me] = jnp.concatenate(
        [as_row(l_total)]
        + [as_row(k_total[h * LANES : (h + 1) * LANES]) for h in range(comps // LANES)]
        + [jnp.zeros((7 - comps // LANES, LANES), F32)],
        axis=0,
    )

    def reduce_and_send():
        gathered[me] = part[tile(mine), :]
        wait_bytes(gathered.at[pl.ds(0, ndev - 1)], rsem.at[7])
        c2[tile(mine), :] = jnp.sum(gathered[...], axis=0)

        @pl.loop(1, ndev)
        def _(hop):
            to = dev(lax.rem(me + hop, ndev))
            remote(c2.at[tile(mine)], c2.at[tile(mine)], 8, to).start()

    if stride == 1:
        reduce_and_send()
    else:
        pl.when(owner)(reduce_and_send)

    @pl.loop(1, ndev)
    def _(hop):
        remote(sums.at[me], sums.at[me], 9, dev(lax.rem(me + hop, ndev))).start()

    if stride == 1:
        wait_bytes(c2.at[pl.ds(0, 8 * (tiles - 1))], rsem.at[8])
    else:

        @pl.when(owner)
        def _():
            wait_bytes(c2.at[pl.ds(0, 8 * (tiles - 1))], rsem.at[8])

        @pl.when(jnp.logical_not(owner))
        def _():
            wait_bytes(c2, rsem.at[8])

    coef_o[...] = jnp.concatenate(
        [c2[pl.ds(h * samples, samples), :] for h in range(comps // LANES)], axis=1
    )
    wait_bytes(sums.at[pl.ds(0, ndev - 1)], rsem.at[9])
    part_mean = jnp.sum(sums[...], axis=0) * (1.0 / ndev)

    def earlier(q, acc):
        return acc + jnp.where(q < me, 1.0, 0.0) * (sums[q] - part_mean)

    level_o[:8, :] = part_mean
    level_o[8:, :] = lax.fori_loop(
        0, ndev, earlier, jnp.zeros((8, LANES), F32), unroll=ndev <= 32
    )

    wait_bytes(send_l.at[pl.ds(0, nb - 1)], ssem.at[0])
    for copy in halos + near:
        copy.wait_send()
    wait_bytes(sums.at[pl.ds(0, ndev - 1)], ssem.at[9])
    if stride == 1:
        wait_bytes(part.at[pl.ds(0, 8 * (tiles - 1))], ssem.at[7])
        wait_bytes(gathered.at[pl.ds(0, ndev - 1)], ssem.at[8])
    else:

        @pl.when(owner)
        def _():
            wait_bytes(part.at[pl.ds(0, 8 * (tiles - 1))], ssem.at[7])
            wait_bytes(gathered.at[pl.ds(0, ndev - 1)], ssem.at[8])

        @pl.when(jnp.logical_not(owner))
        def _():
            wait_bytes(part, ssem.at[7])


def finish(total_bins, coef_i, smooth_i, skh, skl, level, coef_o, smooth_o, bridge_o):
    samples, bin_dev = smooth_o.shape
    comps = skh.shape[0]
    eye = iota((LANES, LANES), 0) == iota((LANES, LANES), 1)
    coef = coef_i[...]
    coef_o[...] = coef

    def resolve(rows):
        level = jnp.where(eye, jnp.broadcast_to(rows[:1], (LANES, LANES)), 0.0)
        for h in range(comps // LANES):
            level = level - coef[:, h * LANES : (h + 1) * LANES] * rows[h + 1 : h + 2]
        return jnp.sum(level, axis=1, keepdims=True)

    mean = resolve(level[:8, :]) * (1.0 / bin_dev)
    carry = resolve(level[8:, :])
    c_high, c_low = split(coef)
    wide = 2 * LANES
    ones = jnp.where(iota((wide, wide), 0) <= iota((wide, wide), 1), 1.0, 0.0).astype(BF16)
    scale = 1.0 / math.sqrt(total_bins)
    runs = []
    for m in range(bin_dev // wide):
        window = pl.ds(m * wide, wide)
        value = smooth_i[:, window] - (
            mm(c_high, skh[:, window]) + mm(c_low, skh[:, window]) + mm(c_high, skl[:, window])
        )
        smooth_o[:, window] = value
        v_high, v_low = split(value - mean)
        runs.append(mm(v_high, ones) + mm(v_low, ones))
    for m, run in enumerate(runs):
        bridge_o[:, pl.ds(m * wide, wide)] = (run + carry) * scale
        carry = carry + run[:, wide - 1 :]


def in_hbm(x):
    return pltpu.with_memory_space_constraint(x, pltpu.HBM)


def solution(mesh):
    nseg, nb = mesh.shape["seg"], mesh.shape["bin"]
    ndev = nseg * nb

    def per_device(lanes, targets, valid, panel, comp, kern, starts):
        samples = lanes.shape[1]
        comps, bin_dev = comp.shape
        layers, ntaps = kern.shape[:2]
        ext = bin_dev + 2 * LANES
        bands = 3 * (bin_dev // LANES) + 2
        vmem, smem = pltpu.VMEM, pltpu.SMEM
        whole = pl.BlockSpec(memory_space=vmem)
        away = pl.BlockSpec(memory_space=pltpu.HBM)
        sds = jax.ShapeDtypeStruct
        coef, smooth, skh, skl, level = pl.pallas_call(
            functools.partial(body, nseg, nb),
            out_shape=(
                sds((samples, comps), F32),
                sds((samples, bin_dev), F32),
                sds((comps, bin_dev), BF16),
                sds((comps, bin_dev), BF16),
                sds((16, LANES), F32),
            ),
            in_specs=[away] * 7,
            out_specs=(whole,) * 5,
            scratch_shapes=[
                smem(targets.shape, jnp.int32),
                smem(valid.shape, jnp.int32),
                smem(starts.shape, jnp.int32),
                vmem(lanes.shape, BF16),
                vmem((1, bin_dev), F32),
                vmem((nb, samples + 16, LANES), BF16),
                vmem((nb, samples + 16, LANES), BF16),
                vmem((comps, ext), F32),
                vmem((layers, ntaps, ext), F32),
                vmem((samples, ext), F32),
                vmem((comps, ext), BF16),
                vmem((comps, ext), BF16),
                vmem((samples, ext), BF16),
                vmem((samples, ext), BF16),
                vmem((comps, ext), BF16),
                vmem((comps, ext), BF16),
                vmem((comps, ext), BF16),
                vmem((comps, ext), BF16),
                vmem((bands, 2 * LANES, 2 * LANES), BF16),
                vmem((samples * comps // LANES, LANES), F32),
                vmem((ndev, 8, LANES), F32),
                vmem((samples * comps // LANES, LANES), F32),
                vmem((ndev, 8, LANES), F32),
                pltpu.SemaphoreType.DMA((10,)),
                pltpu.SemaphoreType.DMA((10,)),
                pltpu.SemaphoreType.DMA((7,)),
            ],
            compiler_params=pltpu.CompilerParams(
                collective_id=0, has_side_effects=True, vmem_limit_bytes=40 << 20
            ),
        )(*map(in_hbm, (targets, valid, starts, lanes, panel.reshape(1, bin_dev), comp, kern)))
        return pl.pallas_call(
            functools.partial(finish, bin_dev * ndev),
            out_shape=(
                sds((samples, comps), F32),
                sds((samples, bin_dev), F32),
                sds((samples, bin_dev), F32),
            ),
            in_specs=[whole] * 5,
            out_specs=(whole,) * 3,
            compiler_params=pltpu.CompilerParams(vmem_limit_bytes=16 << 20),
        )(coef, smooth, skh, skl, level)

    in_specs = (
        P(("seg", "bin"), None, None),
        P(("seg", "bin")),
        P(("seg", "bin")),
        P(("seg", "bin")),
        P(None, ("seg", "bin")),
        P(None, None, ("seg", "bin")),
        P(),
    )
    out_specs = (P(), P(None, ("seg", "bin")), P(None, ("seg", "bin")))
    return jax.shard_map(
        per_device, mesh=mesh, in_specs=in_specs, out_specs=out_specs, check_vma=False
    )
```

```python
import functools
import math

import jax
import jax.numpy as jnp
from jax import lax
from jax.experimental import pallas as pl
from jax.experimental.pallas import tpu as pltpu
from jax.sharding import PartitionSpec as P

MESH = pl.DeviceIdType.MESH
F32, BF16 = jnp.float32, jnp.bfloat16
LANES = 128


def split(x):
    high = x.astype(BF16)
    return high, (x - high.astype(F32)).astype(BF16)


def mm(a, b, contract=(1, 0)):
    return lax.dot_general(
        a, b, (((contract[0],), (contract[1],)), ((), ())), preferred_element_type=F32
    )


def iota(shape, dim):
    return lax.broadcasted_iota(jnp.int32, shape, dim)


def wait_bytes(ref, sem):
    pltpu.make_async_copy(ref, ref, sem).wait()


def body(
    nseg, nb, targets_h, valid_h, starts_h, lanes_h, panel_h, comp, kern,
    coef_o, smooth_o, skh, skl, level_o,
    targets, valid, starts, lanes, panel,
    send_l, recv_l, kx, taps, lrx, kh, kl, lh, ll, ah, al, bh, bl,
    weights, part, gathered, crossed, c2, sums, kout, kin, ssem, rsem, lsem,
):
    ndev = nseg * nb
    seg, place = lax.axis_index("seg"), lax.axis_index("bin")
    me = seg * nb + place
    samples, bin_dev = smooth_o.shape
    comps = kx.shape[0]
    blocks = bin_dev // LANES
    total_bins = bin_dev * ndev
    first = me * bin_dev
    ntaps = kern.shape[1]
    half = (ntaps - 1) // 2

    def dev(flat):
        return (lax.div(flat, nb), lax.rem(flat, nb))

    def remote(src, dst, which, device):
        return pltpu.make_async_remote_copy(
            src_ref=src, dst_ref=dst, send_sem=ssem.at[which], recv_sem=rsem.at[which],
            device_id=device, device_id_type=MESH,
        )

    barrier = pltpu.get_barrier_semaphore()

    def each(start, stop, do):
        if stop - start <= 8:
            for hop in range(start, stop):
                do(hop)
        else:
            pl.loop(start, stop)(do)

    def bin_peer(hop):
        return (seg, lax.rem(place + hop, nb))

    def seg_peer(hop):
        return (lax.rem(seg + hop, nseg), place)

    right, left = dev(lax.rem(me + 1, ndev)), dev(lax.rem(me + ndev - 1, ndev))

    def greet(device):
        pl.semaphore_signal(barrier, inc=1, device_id=device, device_id_type=MESH)

    each(1, nb, lambda hop: greet(bin_peer(hop)))
    each(1, nseg, lambda hop: greet(seg_peer(hop)))
    greet(right)
    greet(left)

    fetched = [
        pltpu.make_async_copy(src, dst, lsem.at[i + 2])
        for i, (src, dst) in enumerate(
            (
                (valid_h, valid), (targets_h, targets), (lanes_h, lanes),
                (starts_h, starts), (panel_h, panel),
            )
        )
    ]
    for copy in fetched:
        copy.start()
    own_k = pltpu.make_async_copy(comp, kx.at[:, pl.ds(LANES, bin_dev)], lsem.at[0])
    own_k.start()
    own_t = pltpu.make_async_copy(kern, taps.at[:, :, pl.ds(LANES, bin_dev)], lsem.at[1])
    own_t.start()

    for copy in fetched:
        copy.wait()

    @pl.loop(0, nb)
    def _(r):
        keep = iota((samples, LANES), 1) < valid[r]
        send_l[r, :samples, :] = jnp.where(keep, lanes[r].astype(F32), 0.0).astype(BF16)
        mark = jnp.full((16, LANES), targets[r], jnp.int32).astype(F32)
        send_l[r, samples:, :] = mark.astype(BF16)

    pl.semaphore_wait(barrier, nb + nseg)

    def exchange(hop):
        to = bin_peer(hop)
        remote(send_l.at[to[1]], recv_l.at[place], 0, to).start()

    each(1, nb, exchange)
    low, high = pl.ds(0, LANES), pl.ds(bin_dev + LANES, LANES)
    head, tail = pl.ds(0, LANES), pl.ds(bin_dev - LANES, LANES)
    halos = [
        remote(kern.at[pl.ds(0, 2), :, tail], taps.at[pl.ds(0, 2), :, low], 1, right),
        remote(kern.at[pl.ds(0, 2), :, head], taps.at[pl.ds(0, 2), :, high], 2, left),
        remote(kout.at[0], kin.at[0], 3, right),
        remote(kout.at[1], kin.at[1], 4, left),
    ]
    for copy in halos[:2]:
        copy.start()
    own_k.wait()
    lower_half = iota((LANES, LANES), 1) < LANES // 2
    first_block, last_block = pl.ds(LANES, LANES), pl.ds(bin_dev, LANES)
    kout[0] = jnp.where(
        lower_half, pltpu.roll(kx[LANES:, last_block], LANES // 2, 1), kx[:LANES, last_block]
    )
    kout[1] = jnp.where(
        lower_half, kx[:LANES, first_block], pltpu.roll(kx[LANES:, first_block], LANES // 2, 1)
    )
    for copy in halos[2:]:
        copy.start()

    recv_l[place] = send_l[place]

    own_t.wait()
    halos[0].wait_recv()
    halos[1].wait_recv()

    def band(layer, m, offset, top):
        if offset == LANES:
            columns = pl.ds(pl.multiple_of((m + 1) * LANES, LANES), LANES)
            upper = taps[layer, : 2 * half, columns]
            last = taps[layer, 2 * half : ntaps, columns]
        else:
            columns = pl.ds(pl.multiple_of(m * LANES, LANES), 2 * LANES)
            upper = taps[layer, : 2 * half, columns]
            last = taps[layer, 2 * half : ntaps, columns]
        last = jnp.broadcast_to(last, (8, last.shape[1]))
        last = jnp.where(iota(last.shape, 0) == 0, last, 0.0)
        rows = jnp.concatenate([upper, last], axis=0)
        if offset != LANES:
            rows = pltpu.roll(rows, 2 * LANES - offset, 1)[:, :LANES]
        position = first - LANES + offset + m * LANES + iota((8, LANES), 1)
        lower = jnp.full((8, LANES), total_bins, jnp.int32)
        upto = jnp.where(position < total_bins, total_bins, -1)
        count = starts.shape[0]
        for k in range(count):
            lower = jnp.where(starts[k] <= position, starts[k], lower)
        for k in range(count - 1, -1, -1):
            upto = jnp.where(starts[k] > position, starts[k], upto)
        tall = rows.shape[0]
        source = position[:1] + iota((tall, LANES), 0) - half
        inside = (source >= lower[:1]) & (source < upto[:1])
        rows = jnp.where(inside, rows, 0.0)
        lane = iota((1, LANES), 1)
        step = 1
        while step < LANES:
            if step < 8:
                moved = pltpu.roll(rows, step, 0)
                still = rows
            else:
                pad = jnp.zeros((step, LANES), F32)
                moved = jnp.concatenate([pad, rows], axis=0)
                still = jnp.concatenate([rows, pad], axis=0)
            chosen = jnp.broadcast_to((lane & step) != 0, moved.shape)
            rows = jnp.where(chosen, moved, still)
            step *= 2
        rest = 2 * LANES - rows.shape[0] - top
        pieces = [rows, jnp.zeros((rest, LANES), F32)]
        if top:
            pieces = [jnp.zeros((top, LANES), F32)] + pieces
        return split(jnp.concatenate(pieces, axis=0))

    plan = (
        (0, LANES - 2 * half, LANES - 3 * half, 0, blocks + 1),
        (1, LANES - half, 0, blocks + 1, blocks + 1),
        (2, LANES, 0, 2 * blocks + 2, blocks),
    )
    for layer, offset, top, base, many in plan:

        @pl.loop(0, many)
        def _(m, layer=layer, offset=offset, top=top, base=base):
            w_high, w_low = band(layer, m, offset, top)
            weights[base + m, :, :LANES] = w_high
            weights[base + m, :, LANES:] = w_low

    def smooth_pass(src_high, src_low, m, base):
        window = pl.ds(m * LANES, 2 * LANES)
        both = mm(src_high[:, window], weights[base + m])
        return both[:, :LANES] + both[:, LANES:] + mm(
            src_low[:, window], weights[base + m, :, :LANES]
        )

    def smooth_first(src, mid, rows, which):
        for m in which:
            out = split(smooth_pass(src[0], src[1], m, plan[0][3]))
            for ref, value in zip(mid, out):
                ref[:rows, pl.ds(m * LANES, LANES)] = value

    def smooth_rest(mid, end, rows, store):
        for m in range(blocks + 1):
            out = split(
                smooth_pass(mid[0].at[:rows], mid[1].at[:rows], m, plan[1][3])
            )
            for ref, value in zip(end, out):
                ref[:rows, pl.ds(m * LANES, LANES)] = value
        total = jnp.zeros((rows, LANES), F32)
        for m in range(blocks):
            out = smooth_pass(end[0].at[:rows], end[1].at[:rows], m, plan[2][3])
            store(m, out)
            total = total + out
        return jnp.sum(total, axis=1, keepdims=True)

    eye = iota((LANES, LANES), 0) == iota((LANES, LANES), 1)

    def as_row(column):
        return jnp.sum(jnp.where(eye, column, 0.0), axis=0, keepdims=True)

    own = pl.ds(LANES, bin_dev)
    for ref in (ah, al, bh, bl):
        ref[:, pl.ds(bin_dev + LANES, LANES)] = jnp.zeros((comps, LANES), BF16)
    kh[:, own], kl[:, own] = split(kx[:, own])
    smooth_first((kh, kl), (ah, al), comps, range(1, blocks))

    def store_k(m, out):
        window = pl.ds(m * LANES, LANES)
        skh[:, window], skl[:, window] = split(out)

    wait_bytes(recv_l.at[pl.ds(0, nb - 1)], rsem.at[0])
    for b in range(blocks):

        def add(r, acc):
            mark = recv_l[r, samples : samples + 16, :].astype(F32)[:1]
            return acc + jnp.where(
                jnp.broadcast_to(mark == float(b), acc.shape),
                recv_l[r, :samples, :].astype(F32), 0.0,
            )

        cover = lax.fori_loop(0, nb, add, jnp.zeros((samples, LANES), F32), unroll=nb <= 8)
        window = pl.ds(b * LANES, LANES)
        lrx[:, pl.ds((b + 1) * LANES, LANES)] = jnp.log(cover + 1.0) - panel[:, window]

    near = [
        remote(lrx.at[:, pl.ds(bin_dev, LANES)], lrx.at[:, low], 5, right),
        remote(lrx.at[:, pl.ds(LANES, LANES)], lrx.at[:, high], 6, left),
    ]
    for copy in near:
        copy.start()

    lh[:, own], ll[:, own] = split(lrx[:, own])
    terms = (
        mm(lh[:, own], kh[:, own], (1, 1))
        + mm(ll[:, own], kh[:, own], (1, 1))
        + mm(lh[:, own], kl[:, own], (1, 1))
    )
    for h in range(comps // LANES):
        part[pl.ds(h * samples, samples), :] = terms[:, h * LANES : (h + 1) * LANES]

    rows = max(8, part.shape[0] // nb)
    chunks = part.shape[0] // rows
    stride = nb // chunks
    mine = lax.div(place, stride)
    owner = lax.rem(place, stride) == 0

    def chunk(j):
        return pl.ds(pl.multiple_of(j * rows, 8), rows)

    def on_owner(do):
        if stride == 1:
            do()
        else:
            pl.when(owner)(do)

    def off_owner(do):
        if stride > 1:
            pl.when(jnp.logical_not(owner))(do)

    def spread(hop):
        j = lax.rem(mine + hop, chunks)
        copy = remote(part.at[chunk(j)], gathered.at[place], 7, (seg, j * stride))
        if stride == 1:
            copy.start()
        else:
            pl.when(j * stride != place)(copy.start)

    each(1 if stride == 1 else 0, chunks, spread)

    halos[2].wait_recv()
    halos[3].wait_recv()
    for side, edge in enumerate((low, high)):
        kh[:LANES, edge], kl[:LANES, edge] = split(kin[side])
        kh[LANES:, edge], kl[LANES:, edge] = split(pltpu.roll(kin[side], LANES // 2, 1))
    smooth_first((kh, kl), (ah, al), comps, (0, blocks))
    k_total = smooth_rest((ah, al), (bh, bl), comps, store_k)

    def reduce_and_cross():
        gathered[place] = part[chunk(mine), :]
        wait_bytes(gathered.at[pl.ds(0, nb - 1)], rsem.at[7])
        crossed[seg] = jnp.sum(gathered[...], axis=0)
        each(1, nseg, lambda hop: remote(
            crossed.at[seg], crossed.at[seg], 10, seg_peer(hop)
        ).start())

    on_owner(reduce_and_cross)
    for copy in near:
        copy.wait_recv()
    for edge in (low, high):
        lh[:, edge], ll[:, edge] = split(lrx[:, edge])

    def store_l(m, out):
        smooth_o[:, pl.ds(m * LANES, LANES)] = out

    smooth_first((lh, ll), (ah, al), samples, range(blocks + 1))
    l_total = smooth_rest((ah, al), (bh, bl), samples, store_l)
    sums[me] = jnp.concatenate(
        [as_row(l_total)]
        + [as_row(k_total[h * LANES : (h + 1) * LANES]) for h in range(comps // LANES)]
        + [jnp.zeros((7 - comps // LANES, LANES), F32)],
        axis=0,
    )
    each(1, nb, lambda hop: remote(sums.at[me], sums.at[me], 9, bin_peer(hop)).start())

    def add_and_return():
        wait_bytes(crossed.at[pl.ds(0, nseg - 1)], rsem.at[10])
        c2[chunk(mine), :] = jnp.sum(crossed[...], axis=0)
        each(1, nb, lambda hop: remote(
            c2.at[chunk(mine)], c2.at[chunk(mine)], 8, bin_peer(hop)
        ).start())

    on_owner(add_and_return)
    wait_bytes(sums.at[pl.ds(0, nb - 1)], rsem.at[9])
    stretch = pl.ds(pl.multiple_of(seg * nb, nb), nb)
    each(1, nseg, lambda hop: remote(
        sums.at[stretch], sums.at[stretch], 11, seg_peer(hop)
    ).start())
    on_owner(lambda: wait_bytes(c2.at[pl.ds(0, rows * (chunks - 1))], rsem.at[8]))
    off_owner(lambda: wait_bytes(c2, rsem.at[8]))
    coef_o[...] = jnp.concatenate(
        [c2[pl.ds(h * samples, samples), :] for h in range(comps // LANES)], axis=1
    )
    wait_bytes(sums.at[pl.ds(0, ndev - nb)], rsem.at[11])
    part_mean = jnp.sum(sums[...], axis=0) * (1.0 / ndev)

    def earlier(q, acc):
        return acc + jnp.where(q < me, 1.0, 0.0) * (sums[q] - part_mean)

    level_o[:8, :] = part_mean
    level_o[8:, :] = lax.fori_loop(
        0, ndev, earlier, jnp.zeros((8, LANES), F32), unroll=ndev <= 32
    )

    wait_bytes(send_l.at[pl.ds(0, nb - 1)], ssem.at[0])
    for copy in halos + near:
        copy.wait_send()
    wait_bytes(sums.at[pl.ds(0, nb - 1)], ssem.at[9])
    wait_bytes(sums.at[pl.ds(0, ndev - nb)], ssem.at[11])

    def drain():
        wait_bytes(part.at[pl.ds(0, rows * (chunks - 1))], ssem.at[7])
        wait_bytes(gathered.at[pl.ds(0, nb - 1)], ssem.at[8])
        wait_bytes(crossed.at[pl.ds(0, nseg - 1)], ssem.at[10])

    on_owner(drain)
    off_owner(lambda: wait_bytes(part, ssem.at[7]))


def finish(total_bins, coef_i, smooth_i, skh, skl, level, coef_o, smooth_o, bridge_o):
    samples, bin_dev = smooth_o.shape
    comps = skh.shape[0]
    eye = iota((LANES, LANES), 0) == iota((LANES, LANES), 1)
    coef = coef_i[...]
    coef_o[...] = coef

    def resolve(rows):
        level = jnp.where(eye, jnp.broadcast_to(rows[:1], (LANES, LANES)), 0.0)
        for h in range(comps // LANES):
            level = level - coef[:, h * LANES : (h + 1) * LANES] * rows[h + 1 : h + 2]
        return jnp.sum(level, axis=1, keepdims=True)

    mean = resolve(level[:8, :]) * (1.0 / bin_dev)
    carry = resolve(level[8:, :])
    c_high, c_low = split(coef)
    wide = 2 * LANES
    ones = jnp.where(iota((wide, wide), 0) <= iota((wide, wide), 1), 1.0, 0.0).astype(BF16)
    scale = 1.0 / math.sqrt(total_bins)
    runs = []
    for m in range(bin_dev // wide):
        window = pl.ds(m * wide, wide)
        value = smooth_i[:, window] - (
            mm(c_high, skh[:, window]) + mm(c_low, skh[:, window]) + mm(c_high, skl[:, window])
        )
        smooth_o[:, window] = value
        v_high, v_low = split(value - mean)
        runs.append(mm(v_high, ones) + mm(v_low, ones))
    for m, run in enumerate(runs):
        bridge_o[:, pl.ds(m * wide, wide)] = (run + carry) * scale
        carry = carry + run[:, wide - 1 :]


def in_hbm(x):
    return pltpu.with_memory_space_constraint(x, pltpu.HBM)


def solution(mesh):
    nseg, nb = mesh.shape["seg"], mesh.shape["bin"]
    ndev = nseg * nb

    def per_device(lanes, targets, valid, panel, comp, kern, starts):
        samples = lanes.shape[1]
        comps, bin_dev = comp.shape
        layers, ntaps = kern.shape[:2]
        ext = bin_dev + 2 * LANES
        flat = samples * comps // LANES
        bands = 3 * (bin_dev // LANES) + 2
        vmem, smem = pltpu.VMEM, pltpu.SMEM
        whole = pl.BlockSpec(memory_space=vmem)
        away = pl.BlockSpec(memory_space=pltpu.HBM)
        sds = jax.ShapeDtypeStruct
        coef, smooth, skh, skl, level = pl.pallas_call(
            functools.partial(body, nseg, nb),
            out_shape=(
                sds((samples, comps), F32),
                sds((samples, bin_dev), F32),
                sds((comps, bin_dev), BF16),
                sds((comps, bin_dev), BF16),
                sds((16, LANES), F32),
            ),
            in_specs=[away] * 7,
            out_specs=(whole,) * 5,
            scratch_shapes=[
                smem(targets.shape, jnp.int32),
                smem(valid.shape, jnp.int32),
                smem(starts.shape, jnp.int32),
                vmem(lanes.shape, BF16),
                vmem((1, bin_dev), F32),
                vmem((nb, samples + 16, LANES), BF16),
                vmem((nb, samples + 16, LANES), BF16),
                vmem((comps, ext), F32),
                vmem((layers, ntaps, ext), F32),
                vmem((samples, ext), F32),
                vmem((comps, ext), BF16),
                vmem((comps, ext), BF16),
                vmem((samples, ext), BF16),
                vmem((samples, ext), BF16),
                vmem((comps, ext), BF16),
                vmem((comps, ext), BF16),
                vmem((comps, ext), BF16),
                vmem((comps, ext), BF16),
                vmem((bands, 2 * LANES, 2 * LANES), BF16),
                vmem((flat, LANES), F32),
                vmem((nb, max(8, flat // nb), LANES), F32),
                vmem((nseg, max(8, flat // nb), LANES), F32),
                vmem((flat, LANES), F32),
                vmem((ndev, 8, LANES), F32),
                vmem((2, LANES, LANES), F32),
                vmem((2, LANES, LANES), F32),
                pltpu.SemaphoreType.DMA((12,)),
                pltpu.SemaphoreType.DMA((12,)),
                pltpu.SemaphoreType.DMA((7,)),
            ],
            compiler_params=pltpu.CompilerParams(
                collective_id=0, has_side_effects=True, vmem_limit_bytes=40 << 20
            ),
        )(*map(in_hbm, (targets, valid, starts, lanes, panel.reshape(1, bin_dev), comp, kern)))
        return pl.pallas_call(
            functools.partial(finish, bin_dev * ndev),
            out_shape=(
                sds((samples, comps), F32),
                sds((samples, bin_dev), F32),
                sds((samples, bin_dev), F32),
            ),
            in_specs=[whole] * 5,
            out_specs=(whole,) * 3,
            compiler_params=pltpu.CompilerParams(vmem_limit_bytes=16 << 20),
        )(coef, smooth, skh, skl, level)

    in_specs = (
        P(("seg", "bin"), None, None),
        P(("seg", "bin")),
        P(("seg", "bin")),
        P(("seg", "bin")),
        P(None, ("seg", "bin")),
        P(None, None, ("seg", "bin")),
        P(),
    )
    out_specs = (P(), P(None, ("seg", "bin")), P(None, ("seg", "bin")))
    return jax.shard_map(
        per_device, mesh=mesh, in_specs=in_specs, out_specs=out_specs, check_vma=False
    )
```

```python
import functools
import math

import jax
import jax.numpy as jnp
from jax import lax
from jax.experimental import pallas as pl
from jax.experimental.pallas import tpu as pltpu
from jax.sharding import PartitionSpec as P

MESH = pl.DeviceIdType.MESH
F32, BF16 = jnp.float32, jnp.bfloat16
LANES = 128


def split(x):
    high = x.astype(BF16)
    return high, (x - high.astype(F32)).astype(BF16)


def mm(a, b, contract=(1, 0)):
    return lax.dot_general(
        a, b, (((contract[0],), (contract[1],)), ((), ())), preferred_element_type=F32
    )


def iota(shape, dim):
    return lax.broadcasted_iota(jnp.int32, shape, dim)


def wait_bytes(ref, sem):
    pltpu.make_async_copy(ref, ref, sem).wait()


def body(
    nseg, nb, targets_h, valid_h, starts_h, lanes_h, panel_h, comp, kern,
    coef_o, smooth_o, skh, skl, level_o,
    targets, valid, starts, lanes, panel,
    send_l, recv_l, kx, taps, lrx, kh, kl, lh, ll, ah, al, bh, bl,
    weights, part, gathered, crossed, c2, sums, kout, kin, ssem, rsem, lsem,
):
    ndev = nseg * nb
    seg, place = lax.axis_index("seg"), lax.axis_index("bin")
    me = seg * nb + place
    samples, bin_dev = smooth_o.shape
    comps = kx.shape[0]
    blocks = bin_dev // LANES
    total_bins = bin_dev * ndev
    first = me * bin_dev
    ntaps = kern.shape[1]
    half = (ntaps - 1) // 2

    def dev(flat):
        return (lax.div(flat, nb), lax.rem(flat, nb))

    def remote(src, dst, which, device):
        return pltpu.make_async_remote_copy(
            src_ref=src, dst_ref=dst, send_sem=ssem.at[which], recv_sem=rsem.at[which],
            device_id=device, device_id_type=MESH,
        )

    barrier = pltpu.get_barrier_semaphore()

    def each(start, stop, do):
        if stop - start <= 8:
            for hop in range(start, stop):
                do(hop)
        else:
            pl.loop(start, stop)(do)

    def bin_peer(hop):
        return (seg, lax.rem(place + hop, nb))

    def seg_peer(hop):
        return (lax.rem(seg + hop, nseg), place)

    right, left = dev(lax.rem(me + 1, ndev)), dev(lax.rem(me + ndev - 1, ndev))

    def greet(device):
        pl.semaphore_signal(barrier, inc=1, device_id=device, device_id_type=MESH)

    each(1, nb, lambda hop: greet(bin_peer(hop)))
    each(1, nseg, lambda hop: greet(seg_peer(hop)))
    greet(right)
    greet(left)

    fetched = [
        pltpu.make_async_copy(src, dst, lsem.at[i + 2])
        for i, (src, dst) in enumerate(
            (
                (valid_h, valid), (targets_h, targets), (lanes_h, lanes),
                (starts_h, starts), (panel_h, panel),
            )
        )
    ]
    for copy in fetched:
        copy.start()
    own_k = pltpu.make_async_copy(comp, kx.at[:, pl.ds(LANES, bin_dev)], lsem.at[0])
    own_k.start()
    own_t = pltpu.make_async_copy(kern, taps.at[:, :, pl.ds(LANES, bin_dev)], lsem.at[1])
    own_t.start()

    for copy in fetched[:3]:
        copy.wait()

    def mask(r):
        keep = iota((samples, LANES), 1) < valid[r]
        send_l[r, :samples, :] = jnp.where(keep, lanes[r].astype(F32), 0.0).astype(BF16)
        mark = jnp.full((16, LANES), targets[r], jnp.int32).astype(F32)
        send_l[r, samples:, :] = mark.astype(BF16)

    each(0, nb, mask)
    for copy in fetched[3:]:
        copy.wait()

    pl.semaphore_wait(barrier, nb + nseg)

    def exchange(hop):
        to = bin_peer(hop)
        remote(send_l.at[to[1]], recv_l.at[place], 0, to).start()

    each(1, nb, exchange)
    low, high = pl.ds(0, LANES), pl.ds(bin_dev + LANES, LANES)
    head, tail = pl.ds(0, LANES), pl.ds(bin_dev - LANES, LANES)
    halos = [
        remote(kern.at[pl.ds(0, 2), :, tail], taps.at[pl.ds(0, 2), :, low], 1, right),
        remote(kern.at[pl.ds(0, 2), :, head], taps.at[pl.ds(0, 2), :, high], 2, left),
        remote(kout.at[0], kin.at[0], 3, right),
        remote(kout.at[1], kin.at[1], 4, left),
    ]
    for copy in halos[:2]:
        copy.start()
    own_k.wait()
    lower_half = iota((LANES, LANES), 1) < LANES // 2
    first_block, last_block = pl.ds(LANES, LANES), pl.ds(bin_dev, LANES)
    kout[0] = jnp.where(
        lower_half, pltpu.roll(kx[LANES:, last_block], LANES // 2, 1), kx[:LANES, last_block]
    )
    kout[1] = jnp.where(
        lower_half, kx[:LANES, first_block], pltpu.roll(kx[LANES:, first_block], LANES // 2, 1)
    )
    for copy in halos[2:]:
        copy.start()

    recv_l[place] = send_l[place]

    own_t.wait()
    halos[0].wait_recv()
    halos[1].wait_recv()

    def band(layer, m, offset, top):
        if offset == LANES:
            columns = pl.ds(pl.multiple_of((m + 1) * LANES, LANES), LANES)
            upper = taps[layer, : 2 * half, columns]
            last = taps[layer, 2 * half : ntaps, columns]
        else:
            columns = pl.ds(pl.multiple_of(m * LANES, LANES), 2 * LANES)
            upper = taps[layer, : 2 * half, columns]
            last = taps[layer, 2 * half : ntaps, columns]
        last = jnp.broadcast_to(last, (8, last.shape[1]))
        last = jnp.where(iota(last.shape, 0) == 0, last, 0.0)
        rows = jnp.concatenate([upper, last], axis=0)
        if offset != LANES:
            rows = pltpu.roll(rows, 2 * LANES - offset, 1)[:, :LANES]
        position = first - LANES + offset + m * LANES + iota((8, LANES), 1)
        lower = jnp.full((8, LANES), total_bins, jnp.int32)
        upto = jnp.where(position < total_bins, total_bins, -1)
        count = starts.shape[0]
        for k in range(count):
            lower = jnp.where(starts[k] <= position, starts[k], lower)
        for k in range(count - 1, -1, -1):
            upto = jnp.where(starts[k] > position, starts[k], upto)
        tall = rows.shape[0]
        source = position[:1] + iota((tall, LANES), 0) - half
        inside = (source >= lower[:1]) & (source < upto[:1])
        rows = jnp.where(inside, rows, 0.0)
        lane = iota((1, LANES), 1)
        step = 1
        while step < LANES:
            if step < 8:
                moved = pltpu.roll(rows, step, 0)
                still = rows
            else:
                pad = jnp.zeros((step, LANES), F32)
                moved = jnp.concatenate([pad, rows], axis=0)
                still = jnp.concatenate([rows, pad], axis=0)
            chosen = jnp.broadcast_to((lane & step) != 0, moved.shape)
            rows = jnp.where(chosen, moved, still)
            step *= 2
        rest = 2 * LANES - rows.shape[0] - top
        pieces = [rows, jnp.zeros((rest, LANES), F32)]
        if top:
            pieces = [jnp.zeros((top, LANES), F32)] + pieces
        return split(jnp.concatenate(pieces, axis=0))

    plan = (
        (0, LANES - 2 * half, LANES - 3 * half, 0, blocks + 1),
        (1, LANES - half, 0, blocks + 1, blocks + 1),
        (2, LANES, 0, 2 * blocks + 2, blocks),
    )
    for layer, offset, top, base, many in plan:

        @pl.loop(0, many)
        def _(m, layer=layer, offset=offset, top=top, base=base):
            w_high, w_low = band(layer, m, offset, top)
            weights[base + m, :, :LANES] = w_high
            weights[base + m, :, LANES:] = w_low

    def smooth_pass(src_high, src_low, m, base):
        window = pl.ds(m * LANES, 2 * LANES)
        both = mm(src_high[:, window], weights[base + m])
        return both[:, :LANES] + both[:, LANES:] + mm(
            src_low[:, window], weights[base + m, :, :LANES]
        )

    def smooth_first(src, mid, rows, which):
        for m in which:
            out = split(smooth_pass(src[0], src[1], m, plan[0][3]))
            for ref, value in zip(mid, out):
                ref[:rows, pl.ds(m * LANES, LANES)] = value

    def smooth_rest(mid, end, rows, store):
        for m in range(blocks + 1):
            out = split(
                smooth_pass(mid[0].at[:rows], mid[1].at[:rows], m, plan[1][3])
            )
            for ref, value in zip(end, out):
                ref[:rows, pl.ds(m * LANES, LANES)] = value
        total = jnp.zeros((rows, LANES), F32)
        for m in range(blocks):
            out = smooth_pass(end[0].at[:rows], end[1].at[:rows], m, plan[2][3])
            store(m, out)
            total = total + out
        return jnp.sum(total, axis=1, keepdims=True)

    eye = iota((LANES, LANES), 0) == iota((LANES, LANES), 1)

    def as_row(column):
        return jnp.sum(jnp.where(eye, column, 0.0), axis=0, keepdims=True)

    own = pl.ds(LANES, bin_dev)
    for ref in (ah, al, bh, bl):
        ref[:, pl.ds(bin_dev + LANES, LANES)] = jnp.zeros((comps, LANES), BF16)
    kh[:, own], kl[:, own] = split(kx[:, own])
    smooth_first((kh, kl), (ah, al), comps, range(1, blocks))

    def store_k(m, out):
        window = pl.ds(m * LANES, LANES)
        skh[:, window], skl[:, window] = split(out)

    wait_bytes(recv_l.at[pl.ds(0, nb - 1)], rsem.at[0])
    for b in range(blocks):

        def add(r, acc):
            mark = recv_l[r, samples : samples + 16, :].astype(F32)[:1]
            return acc + jnp.where(
                jnp.broadcast_to(mark == float(b), acc.shape),
                recv_l[r, :samples, :].astype(F32), 0.0,
            )

        cover = lax.fori_loop(0, nb, add, jnp.zeros((samples, LANES), F32), unroll=nb <= 8)
        window = pl.ds(b * LANES, LANES)
        lrx[:, pl.ds((b + 1) * LANES, LANES)] = jnp.log(cover + 1.0) - panel[:, window]

    near = [
        remote(lrx.at[:, pl.ds(bin_dev, LANES)], lrx.at[:, low], 5, right),
        remote(lrx.at[:, pl.ds(LANES, LANES)], lrx.at[:, high], 6, left),
    ]
    for copy in near:
        copy.start()

    lh[:, own], ll[:, own] = split(lrx[:, own])
    terms = (
        mm(lh[:, own], kh[:, own], (1, 1))
        + mm(ll[:, own], kh[:, own], (1, 1))
        + mm(lh[:, own], kl[:, own], (1, 1))
    )
    for h in range(comps // LANES):
        part[pl.ds(h * samples, samples), :] = terms[:, h * LANES : (h + 1) * LANES]

    rows = max(8, part.shape[0] // nb)
    chunks = part.shape[0] // rows
    stride = nb // chunks
    mine = lax.div(place, stride)
    owner = lax.rem(place, stride) == 0

    def chunk(j):
        return pl.ds(pl.multiple_of(j * rows, 8), rows)

    def on_owner(do):
        if stride == 1:
            do()
        else:
            pl.when(owner)(do)

    def off_owner(do):
        if stride > 1:
            pl.when(jnp.logical_not(owner))(do)

    def spread(hop):
        j = lax.rem(mine + hop, chunks)
        copy = remote(part.at[chunk(j)], gathered.at[place], 7, (seg, j * stride))
        if stride == 1:
            copy.start()
        else:
            pl.when(j * stride != place)(copy.start)

    each(1 if stride == 1 else 0, chunks, spread)

    halos[2].wait_recv()
    halos[3].wait_recv()
    for side, edge in enumerate((low, high)):
        kh[:LANES, edge], kl[:LANES, edge] = split(kin[side])
        kh[LANES:, edge], kl[LANES:, edge] = split(pltpu.roll(kin[side], LANES // 2, 1))
    smooth_first((kh, kl), (ah, al), comps, (0, blocks))
    k_total = smooth_rest((ah, al), (bh, bl), comps, store_k)

    def reduce_and_cross():
        gathered[place] = part[chunk(mine), :]
        wait_bytes(gathered.at[pl.ds(0, nb - 1)], rsem.at[7])
        crossed[seg] = jnp.sum(gathered[...], axis=0)
        each(1, nseg, lambda hop: remote(
            crossed.at[seg], crossed.at[seg], 10, seg_peer(hop)
        ).start())

    on_owner(reduce_and_cross)
    for copy in near:
        copy.wait_recv()
    for edge in (low, high):
        lh[:, edge], ll[:, edge] = split(lrx[:, edge])

    def store_l(m, out):
        smooth_o[:, pl.ds(m * LANES, LANES)] = out

    smooth_first((lh, ll), (ah, al), samples, range(blocks + 1))
    l_total = smooth_rest((ah, al), (bh, bl), samples, store_l)
    sums[me] = jnp.concatenate(
        [as_row(l_total)]
        + [as_row(k_total[h * LANES : (h + 1) * LANES]) for h in range(comps // LANES)]
        + [jnp.zeros((7 - comps // LANES, LANES), F32)],
        axis=0,
    )
    each(1, nb, lambda hop: remote(sums.at[me], sums.at[me], 9, bin_peer(hop)).start())

    def add_and_return():
        wait_bytes(crossed.at[pl.ds(0, nseg - 1)], rsem.at[10])
        c2[chunk(mine), :] = jnp.sum(crossed[...], axis=0)
        each(1, nb, lambda hop: remote(
            c2.at[chunk(mine)], c2.at[chunk(mine)], 8, bin_peer(hop)
        ).start())

    on_owner(add_and_return)
    wait_bytes(sums.at[pl.ds(0, nb - 1)], rsem.at[9])
    stretch = pl.ds(pl.multiple_of(seg * nb, nb), nb)
    each(1, nseg, lambda hop: remote(
        sums.at[stretch], sums.at[stretch], 11, seg_peer(hop)
    ).start())
    on_owner(lambda: wait_bytes(c2.at[pl.ds(0, rows * (chunks - 1))], rsem.at[8]))
    off_owner(lambda: wait_bytes(c2, rsem.at[8]))
    coef_o[...] = jnp.concatenate(
        [c2[pl.ds(h * samples, samples), :] for h in range(comps // LANES)], axis=1
    )
    wait_bytes(sums.at[pl.ds(0, ndev - nb)], rsem.at[11])
    part_mean = jnp.sum(sums[...], axis=0) * (1.0 / ndev)

    def earlier(q, acc):
        return acc + jnp.where(q < me, 1.0, 0.0) * (sums[q] - part_mean)

    level_o[:8, :] = part_mean
    level_o[8:, :] = lax.fori_loop(
        0, ndev, earlier, jnp.zeros((8, LANES), F32), unroll=ndev <= 32
    )

    wait_bytes(send_l.at[pl.ds(0, nb - 1)], ssem.at[0])
    for copy in halos + near:
        copy.wait_send()
    wait_bytes(sums.at[pl.ds(0, nb - 1)], ssem.at[9])
    wait_bytes(sums.at[pl.ds(0, ndev - nb)], ssem.at[11])

    def drain():
        wait_bytes(part.at[pl.ds(0, rows * (chunks - 1))], ssem.at[7])
        wait_bytes(gathered.at[pl.ds(0, nb - 1)], ssem.at[8])
        wait_bytes(crossed.at[pl.ds(0, nseg - 1)], ssem.at[10])

    on_owner(drain)
    off_owner(lambda: wait_bytes(part, ssem.at[7]))


def finish(total_bins, coef_i, smooth_i, skh, skl, level, coef_o, smooth_o, bridge_o):
    samples, bin_dev = smooth_o.shape
    comps = skh.shape[0]
    eye = iota((LANES, LANES), 0) == iota((LANES, LANES), 1)
    coef = coef_i[...]
    coef_o[...] = coef

    def resolve(rows):
        level = jnp.where(eye, jnp.broadcast_to(rows[:1], (LANES, LANES)), 0.0)
        for h in range(comps // LANES):
            level = level - coef[:, h * LANES : (h + 1) * LANES] * rows[h + 1 : h + 2]
        return jnp.sum(level, axis=1, keepdims=True)

    mean = resolve(level[:8, :]) * (1.0 / bin_dev)
    carry = resolve(level[8:, :])
    c_high, c_low = split(coef)
    wide = 2 * LANES
    ones = jnp.where(iota((wide, wide), 0) <= iota((wide, wide), 1), 1.0, 0.0).astype(BF16)
    scale = 1.0 / math.sqrt(total_bins)
    runs = []
    for m in range(bin_dev // wide):
        window = pl.ds(m * wide, wide)
        value = smooth_i[:, window] - (
            mm(c_high, skh[:, window]) + mm(c_low, skh[:, window]) + mm(c_high, skl[:, window])
        )
        smooth_o[:, window] = value
        v_high, v_low = split(value - mean)
        runs.append(mm(v_high, ones) + mm(v_low, ones))
    for m, run in enumerate(runs):
        bridge_o[:, pl.ds(m * wide, wide)] = (run + carry) * scale
        carry = carry + run[:, wide - 1 :]


def in_hbm(x):
    return pltpu.with_memory_space_constraint(x, pltpu.HBM)


def solution(mesh):
    nseg, nb = mesh.shape["seg"], mesh.shape["bin"]
    ndev = nseg * nb

    def per_device(lanes, targets, valid, panel, comp, kern, starts):
        samples = lanes.shape[1]
        comps, bin_dev = comp.shape
        layers, ntaps = kern.shape[:2]
        ext = bin_dev + 2 * LANES
        flat = samples * comps // LANES
        bands = 3 * (bin_dev // LANES) + 2
        vmem, smem = pltpu.VMEM, pltpu.SMEM
        whole = pl.BlockSpec(memory_space=vmem)
        away = pl.BlockSpec(memory_space=pltpu.HBM)
        sds = jax.ShapeDtypeStruct
        coef, smooth, skh, skl, level = pl.pallas_call(
            functools.partial(body, nseg, nb),
            out_shape=(
                sds((samples, comps), F32),
                sds((samples, bin_dev), F32),
                sds((comps, bin_dev), BF16),
                sds((comps, bin_dev), BF16),
                sds((16, LANES), F32),
            ),
            in_specs=[away] * 7,
            out_specs=(whole,) * 5,
            scratch_shapes=[
                smem(targets.shape, jnp.int32),
                smem(valid.shape, jnp.int32),
                smem(starts.shape, jnp.int32),
                vmem(lanes.shape, BF16),
                vmem((1, bin_dev), F32),
                vmem((nb, samples + 16, LANES), BF16),
                vmem((nb, samples + 16, LANES), BF16),
                vmem((comps, ext), F32),
                vmem((layers, ntaps, ext), F32),
                vmem((samples, ext), F32),
                vmem((comps, ext), BF16),
                vmem((comps, ext), BF16),
                vmem((samples, ext), BF16),
                vmem((samples, ext), BF16),
                vmem((comps, ext), BF16),
                vmem((comps, ext), BF16),
                vmem((comps, ext), BF16),
                vmem((comps, ext), BF16),
                vmem((bands, 2 * LANES, 2 * LANES), BF16),
                vmem((flat, LANES), F32),
                vmem((nb, max(8, flat // nb), LANES), F32),
                vmem((nseg, max(8, flat // nb), LANES), F32),
                vmem((flat, LANES), F32),
                vmem((ndev, 8, LANES), F32),
                vmem((2, LANES, LANES), F32),
                vmem((2, LANES, LANES), F32),
                pltpu.SemaphoreType.DMA((12,)),
                pltpu.SemaphoreType.DMA((12,)),
                pltpu.SemaphoreType.DMA((7,)),
            ],
            compiler_params=pltpu.CompilerParams(
                collective_id=0, has_side_effects=True, vmem_limit_bytes=40 << 20
            ),
        )(*map(in_hbm, (targets, valid, starts, lanes, panel.reshape(1, bin_dev), comp, kern)))
        return pl.pallas_call(
            functools.partial(finish, bin_dev * ndev),
            out_shape=(
                sds((samples, comps), F32),
                sds((samples, bin_dev), F32),
                sds((samples, bin_dev), F32),
            ),
            in_specs=[whole] * 5,
            out_specs=(whole,) * 3,
            compiler_params=pltpu.CompilerParams(vmem_limit_bytes=16 << 20),
        )(coef, smooth, skh, skl, level)

    in_specs = (
        P(("seg", "bin"), None, None),
        P(("seg", "bin")),
        P(("seg", "bin")),
        P(("seg", "bin")),
        P(None, ("seg", "bin")),
        P(None, None, ("seg", "bin")),
        P(),
    )
    out_specs = (P(), P(None, ("seg", "bin")), P(None, ("seg", "bin")))
    return jax.shard_map(
        per_device, mesh=mesh, in_specs=in_specs, out_specs=out_specs, check_vma=False
    )
```
